512 devices in a mesh: panel: 32 (over z, x_lo, core), case: 16 (over x_hi, y).
Axes of the slice: x: 4 (x_hi: 2, x_lo: 2; x = x_hi * 2 + x_lo), y: 8, z: 8, core: 2. Of those that a mesh axis runs over, the one named last changes fastest.
Arguments:
- strengths: bfloat16 [32, 196608], P('panel', 'case'), may hold values from -6 to 6
- blocks: bfloat16 [16384, 256, 256], P(('panel', 'case')), may hold values from -0.109375 to 0.109375
- pattern: int32 [16384, 3], P(('panel', 'case')), may hold values from -1 to 767, as said below
- level_gain: float32 [8], replicated, may hold values from 0.25 to 2
Outputs:
- forward_one: bfloat16 [32, 196608], P('case', 'panel')
- adjoint_one: bfloat16 [32, 196608], P('panel', 'case')
- forward_two: bfloat16 [32, 196608], P('case', 'panel')
- adjoint_two: bfloat16 [32, 196608], P('panel', 'case')
The draws below stay inside these ranges and needn't reach their ends.
Inputs may be any that keep to these rules, and one draw needn't show every extreme that they name: `pattern`: entries come in runs of 32, one run for each pair of a panel index p and a case index c, ordered with p slowest; a run's row blocks lie in p * 24 to (p + 1) * 24 - 1 and its column blocks in c * 48 to (c + 1) * 48 - 1; no (row block, column block) pair appears twice; levels lie in 0 to 7; an empty slot is (-1, -1, -1), a run holds its stored blocks first and its empty slots after them, every run holds at least one stored block and some run is full.
All inputs are finite; a program needn't handle non-finite values.
Results may differ from the reference program's by a relative error of at most 0.024.
Values may be sent and summed in bfloat16 or wider, within the bound.
A program may use at most 64 MiB of HBM per device.

```python
import math
import jax
import jax.numpy as jnp
from jax import lax

B = 256
CASES = 32
LEVELS = 8
ROWB_DEV = 24
BLK_DEV = 32
COLB_DEV = 48
NBLK = 16384
NPAN = 196608
N_PANEL = 32
N_CASE = 16


def draw_pattern(key, part):
    device_count = N_PANEL * N_CASE
    tile_size = ROWB_DEV * COLB_DEV
    key_order, key_count, key_full, key_level = jax.random.split(jax.random.fold_in(key, 17), 4)
    scores = jax.random.randint(key_order, (device_count, tile_size), 0, 1 << 20)
    scores = scores * tile_size + jnp.arange(tile_size, dtype=jnp.int32)[None, :]
    scores = scores.at[:, tile_size - 1].set(-1)
    order = jnp.argsort(scores, axis=1, stable=True)[:, :BLK_DEV].astype(jnp.int32)
    row_local = order // COLB_DEV
    col_local = order % COLB_DEV
    counts = jax.random.randint(key_count, (device_count,), max(1, BLK_DEV // 4), BLK_DEV + 1)
    full_device = jax.random.randint(key_full, (), 0, device_count)
    counts = jnp.where(jnp.arange(device_count) == full_device, BLK_DEV, counts)
    is_live = jnp.arange(BLK_DEV)[None, :] < counts[:, None]
    device_ids = jnp.arange(device_count, dtype=jnp.int32)
    panel_ids = device_ids // N_CASE
    case_ids = device_ids % N_CASE
    row_block = panel_ids[:, None] * ROWB_DEV + row_local
    col_block = case_ids[:, None] * COLB_DEV + col_local
    level_ids = jax.random.randint(key_level, (device_count, BLK_DEV), 0, LEVELS)
    stacked = jnp.stack([row_block, col_block, level_ids], axis=2)
    stacked = jnp.where(is_live[:, :, None], stacked, -1)
    return stacked.reshape(device_count * BLK_DEV, 3).astype(jnp.int32)


def level_of(own_key, shape, shards, smallest, top_value):
    level, own = 1.0, jax.random.fold_in(own_key, 6)
    for position, parts in shards:
        draws = jnp.exp(jax.random.uniform(jax.random.fold_in(own, position), (parts,), jnp.float32, smallest / len(shards), top_value / len(shards)))
        level = level * jnp.repeat(draws, shape[position] // parts).reshape([-1 if axis == position else 1 for axis in range(len(shape))])
    return level


def centred(key, dims, width, most, cuts=(), held_as=jnp.bfloat16):
    drawn = width * jax.random.normal(key, dims, jnp.float32)
    if cuts:
        drawn = drawn * level_of(key, dims, cuts, -0.22, 0.18)
    return jnp.clip(drawn, -most, most).astype(held_as)


def setup_inputs(seed: int = 0) -> dict:
    arg_keys = jax.random.split(jax.random.key(seed), 5)
    return {
        "strengths": centred(arg_keys[0], (CASES, NPAN), 1.0, 6.0, ((0, 32), (1, 16))),
        "blocks": centred(arg_keys[1], (NBLK, B, B), (B * N_CASE * BLK_DEV * 5 // (8 * ROWB_DEV)) ** -0.5, 0.109375, ((0, 512),)),
        "pattern": draw_pattern(jax.random.fold_in(arg_keys[4], 71), 0),
        "level_gain": jnp.clip(jnp.exp(jax.random.uniform(arg_keys[3], (LEVELS,), jnp.float32, math.log(0.25), math.log(2.0))), 0.25, 2.0),
    }


def level_scale(pattern, level_gain):
    level_ids = jnp.arange(LEVELS, dtype=jnp.int32)
    chosen = jnp.where(pattern[:, 2:3] == level_ids[None, :], level_gain[None, :], jnp.float32(0.0))
    return jnp.sum(chosen, axis=1)


def group_partial(values, group_blocks, group_pattern, group_scale, adjoint):
    running = jnp.zeros((CASES, NPAN), jnp.float32)

    def advance(carry, record):
        tile_block, entries, factor = record
        row_at = jnp.maximum(entries[0], 0).astype(jnp.int32) * B
        col_at = jnp.maximum(entries[1], 0).astype(jnp.int32) * B
        matrix = tile_block.astype(jnp.float32)
        if adjoint:
            source = lax.dynamic_slice_in_dim(values, row_at, B, 1).astype(jnp.float32)
            product_term = jnp.dot(source, matrix, precision=lax.Precision.HIGHEST) * factor
            target = col_at
        else:
            source = lax.dynamic_slice_in_dim(values, col_at, B, 1).astype(jnp.float32)
            product_term = jnp.dot(source, matrix.T, precision=lax.Precision.HIGHEST) * factor
            target = row_at
        current = lax.dynamic_slice_in_dim(carry, target, B, 1)
        carry = lax.dynamic_update_slice_in_dim(carry, current + product_term, target, 1)
        return carry, None

    running, _ = lax.scan(advance, running, (group_blocks, group_pattern, group_scale))
    return running


def apply_matrix(values, blocks, pattern, block_scale, adjoint):
    blocks_runs = blocks.reshape(N_PANEL, N_CASE, BLK_DEV, B, B)
    pattern_runs = pattern.reshape(N_PANEL, N_CASE, BLK_DEV, 3)
    scale_runs = block_scale.reshape(N_PANEL, N_CASE, BLK_DEV)
    group_axis = 0 if adjoint else 1
    group_count = N_PANEL if adjoint else N_CASE

    def one_group(total, group):
        group_blocks = lax.dynamic_index_in_dim(blocks_runs, group, group_axis, keepdims=False).reshape(-1, B, B)
        group_pattern = lax.dynamic_index_in_dim(pattern_runs, group, group_axis, keepdims=False).reshape(-1, 3)
        group_scale = lax.dynamic_index_in_dim(scale_runs, group, group_axis, keepdims=False).reshape(-1)
        partial_value = group_partial(values, group_blocks, group_pattern, group_scale, adjoint)
        rounded = lax.optimization_barrier(partial_value.astype(jnp.bfloat16)).astype(jnp.float32)
        return total + rounded, None

    total, _ = lax.scan(one_group, jnp.zeros((CASES, NPAN), jnp.float32), jnp.arange(group_count, dtype=jnp.int32))
    return total.astype(jnp.bfloat16)


def reference(strengths, blocks, pattern, level_gain):
    block_scale = level_scale(pattern, level_gain)
    forward_one = apply_matrix(strengths, blocks, pattern, block_scale, False)
    adjoint_one = apply_matrix(forward_one, blocks, pattern, block_scale, True)
    forward_two = apply_matrix(adjoint_one, blocks, pattern, block_scale, False)
    adjoint_two = apply_matrix(forward_two, blocks, pattern, block_scale, True)
    return forward_one, adjoint_one, forward_two, adjoint_two
```

```python
import contextlib

import jax
import jax.numpy as jnp
from jax import lax
from jax.experimental import pallas as pl
from jax.experimental.pallas import tpu as pltpu
from jax.sharding import PartitionSpec as P

B = 256
ROWB = 24
COLB = 48
BLK = 32
CASES = 32
LANES = 128
PART = 3
RING = 8
MESH = pl.DeviceIdType.MESH
FAR_FIRST = (4, 3, 5, 2, 6, 1, 7)
NEAR_FIRST = (1, 7, 2, 6, 3, 5, 4)

f32 = jnp.float32
bf16 = jnp.bfloat16


def chunk(ref, q, count=1):
    return ref.at[pl.ds(q * PART, count * PART)]


def read(ref, q):
    return ref[pl.ds(q * PART, PART)].astype(f32)


def stage(name):
    return contextlib.nullcontext()


class Link:
    def __init__(self, send_sem, recv_sem):
        self.send_sem, self.recv_sem = send_sem, recv_sem
        self.used = 0
        self.open = []

    def take(self, count):
        first = self.used
        self.used += count
        return first

    def copy(self, src, dst, slot_out, slot_in, device):
        return pltpu.make_async_remote_copy(
            src_ref=src,
            dst_ref=dst,
            send_sem=self.send_sem.at[slot_out],
            recv_sem=self.recv_sem.at[slot_in],
            device_id=device,
            device_id_type=MESH,
        )

    def send(self, src, dst, slot_out, slot_in, device):
        copy = self.copy(src, dst, slot_out, slot_in, device)
        copy.start()
        self.open.append(copy)

    def arrived(self, dst, slot_in, device):
        self.copy(dst, dst, slot_in, slot_in, device).wait_recv()

    def drain(self):
        for copy in self.open:
            copy.wait_send()
        self.open = []


class Group:
    def __init__(self, ring, pair, core=None):
        (self.i, self.peer), (self.j, self.partner) = ring, pair
        self.core, self.twin = core if core else (None, None)
        self.base = 0 if core is None else self.core * 16

    def at(self, d):
        return lax.rem(self.i + d, RING)


def gather(link, g, buf):
    own_ring = g.base + g.j * RING
    far_ring = g.base + (1 - g.j) * RING
    ring, pair = link.take(RING), link.take(RING)
    twin = link.take(2) if g.twin is not None else None
    mine = chunk(buf, own_ring + g.i)
    link.send(mine, mine, pair, pair, g.partner)
    for d in FAR_FIRST:
        link.send(mine, mine, ring + d, ring + RING - d, g.peer(d))
    for d in NEAR_FIRST:
        piece = chunk(buf, own_ring + g.at(d))
        link.arrived(piece, ring + d, g.peer(d))
        link.send(piece, piece, pair + d, pair + d, g.partner)
    if twin is not None:
        whole = chunk(buf, own_ring, RING)
        link.send(whole, whole, twin, twin, g.twin)
    for d in (0,) + NEAR_FIRST:
        link.arrived(chunk(buf, far_ring + g.at(d)), pair + d, g.partner)
    if twin is not None:
        whole = chunk(buf, far_ring, RING)
        link.send(whole, whole, twin + 1, twin + 1, g.twin)
        other = (1 - g.core) * 16
        link.arrived(chunk(buf, other + g.j * RING, RING), twin, g.twin)
        link.arrived(chunk(buf, other + (1 - g.j) * RING, RING), twin + 1, g.twin)


def scatter(link, g, src, from_twin, joined, from_pair, summed, from_ring):
    if g.twin is not None:
        slots = link.take(2)
        other = (1 - g.core) * 16
        for n, half in enumerate((1 - g.j, g.j)):
            link.send(
                chunk(src, other + half * RING, RING),
                chunk(from_twin, half * RING, RING),
                slots + n,
                slots + n,
                g.twin,
            )

        def join(half):
            def one(t, carry):
                at = half * RING * PART + t
                joined[at] = (
                    src[g.base * PART + at].astype(f32) + from_twin[at].astype(f32)
                ).astype(bf16)
                return carry

            lax.fori_loop(0, RING * PART, one, 0)

        link.arrived(chunk(from_twin, (1 - g.j) * RING, RING), slots, g.twin)
        join(1 - g.j)
    ready = src if g.twin is None else joined
    pair, ring = link.take(RING), link.take(RING)
    far, near = (1 - g.j) * RING, g.j * RING
    for d in FAR_FIRST + (0,):
        link.send(chunk(ready, far + g.at(d)), chunk(from_pair, d), pair + d, pair + d, g.partner)
    if g.twin is not None:
        link.arrived(chunk(from_twin, g.j * RING, RING), slots + 1, g.twin)
        join(g.j)
    for d in FAR_FIRST:
        link.arrived(chunk(from_pair, d), pair + d, g.partner)
        total = read(ready, near + g.at(d)) + read(from_pair, d)
        summed[pl.ds(d * PART, PART)] = total.astype(bf16)
        link.send(
            chunk(summed, d), chunk(from_ring, RING - d), ring + d, ring + RING - d, g.peer(d)
        )
    link.arrived(chunk(from_pair, 0), pair, g.partner)
    total = read(ready, near + g.i) + read(from_pair, 0)
    for d in NEAR_FIRST:
        link.arrived(chunk(from_ring, d), ring + d, g.peer(d))
        total = total + read(from_ring, d)
    return total


def kernel(
    table, scale, strengths, blocks_hbm,
    fwd_one, adj_one, fwd_two, adj_two,
    blocks, rows_in, x_one, x_two, f_one, f_two, y_one, y_two, z_one, z_two,
    terms, wide, flat, twin_buf, join_buf, pair_buf, sum_buf, ring_buf,
    send_sem, recv_sem, load_sem,
):
    p, c = lax.axis_index("panel"), lax.axis_index("case")
    z, x_lo, core = p // 4, lax.rem(p // 2, 2), lax.rem(p, 2)
    x_hi, y = c // RING, lax.rem(c, RING)
    load = pltpu.make_async_copy(blocks_hbm, blocks, load_sem)
    load.start()

    by_panel = Group(
        (z, lambda d: {"panel": lax.rem(z + d, RING) * 4 + x_lo * 2 + core}),
        (x_lo, {"panel": z * 4 + (1 - x_lo) * 2 + core}),
        (core, {"panel": z * 4 + x_lo * 2 + (1 - core)}),
    )
    by_case = Group(
        (y, lambda d: {"case": x_hi * RING + lax.rem(y + d, RING)}),
        (x_hi, {"case": (1 - x_hi) * RING + y}),
    )
    barrier = pltpu.get_barrier_semaphore()
    met = [by_panel.twin, by_panel.partner, by_case.partner]
    met += [g.peer(d) for d in NEAR_FIRST for g in (by_panel, by_case)]
    for device in met:
        pl.semaphore_signal(barrier, inc=1, device_id=device, device_id_type=MESH)

    place = core * 16 + x_lo * RING + z

    for n in range(COLB * 2):
        flat[n : n + 1, :] = strengths[0:1, n * LANES : (n + 1) * LANES].astype(f32)
    for n in range(PART):
        rows_in[place * PART + n] = flat[n * CASES : (n + 1) * CASES, :].astype(bf16)
    terms[BLK] = jnp.zeros((CASES, B), f32)
    with stage("meet"):
        pl.semaphore_wait(barrier, len(met))

    link = Link(send_sem, recv_sem)
    with stage("gath0"):
        gather(link, by_panel, rows_in)

    def widen(t, carry):
        wide[pl.ds(t * CASES, CASES), :] = rows_in[t].astype(f32)
        return carry

    lax.fori_loop(0, COLB * 2, widen, 0)

    def turn(t, carry):
        x_one[t] = wide[pl.ds(t, CASES, stride=COLB * 2), :].astype(bf16)
        return carry

    lax.fori_loop(0, COLB * 2, turn, 0)
    with stage("load"):
        load.wait()

    def product(src, where_from, chained, dims):
        def some(step, carry):
            found = []
            for n in range(4):
                b = step * 4 + n
                at = table[where_from + b] * 2
                operand = jnp.concatenate([src[at], src[at + 1]], axis=1)
                found.append(
                    lax.dot_general(operand, blocks[b], (dims, ((), ())), preferred_element_type=f32)
                    * scale[b]
                )
            for n in range(4):
                b = step * 4 + n
                terms[b] = found[n] + terms[table[chained + b]]
            return carry

        lax.fori_loop(0, BLK // 4, some, 0)

    def forward(src, dst):
        product(src, BLK, 2 * BLK, ((1,), (1,)))

        def out(r, carry):
            total = terms[table[4 * BLK + r]].astype(bf16)
            dst[2 * r] = total[:, :LANES]
            dst[2 * r + 1] = total[:, LANES:]
            return carry

        lax.fori_loop(0, ROWB, out, 0)

    def adjoint(src, dst):
        product(src, 0, 3 * BLK, ((1,), (0,)))

        def out(r, carry):
            total = terms[table[4 * BLK + ROWB + r]]
            if dst is None:
                wide[pl.ds(2 * r, CASES, stride=COLB * 2), :] = total[:, :LANES]
                wide[pl.ds(2 * r + 1, CASES, stride=COLB * 2), :] = total[:, LANES:]
            else:
                total = total.astype(bf16)
                dst[2 * r] = total[:, :LANES]
                dst[2 * r + 1] = total[:, LANES:]
            return carry

        lax.fori_loop(0, COLB, out, 0)

    def pick(src, dst, places, count):
        lane = lax.broadcasted_iota(jnp.int32, (8, CASES), 1)
        line = lax.broadcasted_iota(jnp.int32, (8, CASES), 0)
        chosen = jnp.zeros((8, CASES), f32)
        for n, at in enumerate(places):
            chosen = jnp.where((line == n) & (lane == at), f32(1.0), chosen)
        chosen = chosen.astype(bf16)
        for t in range(count):
            both = jnp.concatenate([src[2 * t], src[2 * t + 1]], axis=1)
            found = jnp.dot(chosen, both, preferred_element_type=f32)
            dst[:, t * B : (t + 1) * B] = found[: len(places)].astype(bf16)

    def place_of(k):
        return lax.rem(k, 2) * 16 + lax.rem(k // 2, 2) * RING + k // 4

    mine = [place_of(2 * c), place_of(2 * c + 1)]

    def reduce_rows(n, src, dst):
        with stage("rs"):
            total = scatter(
                link, by_case, src, None, None, pair_buf.at[n], sum_buf.at[n], ring_buf.at[n]
            )
        with stage("ag"):
            dst[pl.ds(c * PART, PART)] = total.astype(bf16)
            gather(link, by_case, dst)

    with stage("fwd1"):
        forward(x_one, y_one)
    with stage("red1"):
        reduce_rows(0, y_one, f_one)
    with stage("adj1"):
        adjoint(f_one, z_one)
        pick(f_one, fwd_one, mine, ROWB)
    with stage("scat2"):
        total = scatter(
            link, by_panel, z_one, twin_buf.at[0], join_buf.at[0],
            pair_buf.at[1], sum_buf.at[1], ring_buf.at[1],
        )
    with stage("gath2"):
        x_two[pl.ds(place * PART, PART)] = total.astype(bf16)
        gather(link, by_panel, x_two)
    with stage("fwd2"):
        forward(x_two, y_two)
    with stage("red3"):
        reduce_rows(2, y_two, f_two)
    with stage("adj2"):
        adjoint(f_two, None)

        def narrow(t, carry):
            z_two[t] = wide[pl.ds(t * CASES, CASES), :].astype(bf16)
            return carry

        lax.fori_loop(0, COLB * 2, narrow, 0)
        pick(x_two, adj_one, [place], COLB)
        pick(f_two, fwd_two, mine, ROWB)
    with stage("scat4"):
        total = scatter(
            link, by_panel, z_two, twin_buf.at[1], join_buf.at[1],
            pair_buf.at[3], sum_buf.at[3], ring_buf.at[3],
        )
    for n in range(PART):
        flat[n * CASES : (n + 1) * CASES, :] = total[n]
    for n in range(COLB * 2):
        adj_two[0:1, n * LANES : (n + 1) * LANES] = flat[n : n + 1, :].astype(bf16)
    link.drain()


COPIES = 160


def tables(pattern, level_gain):
    level_ids = jnp.arange(level_gain.shape[0], dtype=jnp.int32)
    scale = jnp.sum(
        jnp.where(pattern[:, 2:3] == level_ids[None, :], level_gain[None, :], f32(0.0)), axis=1
    )
    live = pattern[:, 2] >= 0
    row = jnp.where(live, pattern[:, 0] - lax.axis_index("panel") * ROWB, -1)
    col = jnp.where(live, pattern[:, 1] - lax.axis_index("case") * COLB, -1)
    slot = jnp.arange(BLK, dtype=jnp.int32)

    def last(keys, own, before):
        hit = own[:, None] == keys[None, :]
        if before:
            hit = hit & (slot[None, :] < slot[:, None])
        found = jnp.max(jnp.where(hit, slot[None, :], -1), axis=1)
        return jnp.where(found < 0, BLK, found)

    table = jnp.concatenate([
        jnp.maximum(row, 0),
        jnp.maximum(col, 0),
        last(row, row, True),
        last(col, col, True),
        last(row, jnp.arange(ROWB, dtype=jnp.int32), False),
        last(col, jnp.arange(COLB, dtype=jnp.int32), False),
    ])
    return table, scale


def shards(strengths, blocks, pattern, level_gain):
    table, scale = tables(pattern, level_gain)
    V = pltpu.VMEM
    cols = (2 * COLB, CASES, LANES)
    rows = (2 * ROWB, CASES, LANES)
    ring = (RING * PART, CASES, LANES)
    half = (2, 2 * RING * PART, CASES, LANES)
    return pl.pallas_call(
        kernel,
        out_shape=(
            jax.ShapeDtypeStruct((2, ROWB * B), bf16),
            jax.ShapeDtypeStruct((1, COLB * B), bf16),
            jax.ShapeDtypeStruct((2, ROWB * B), bf16),
            jax.ShapeDtypeStruct((1, COLB * B), bf16),
        ),
        in_specs=[
            pl.BlockSpec(memory_space=pltpu.SMEM),
            pl.BlockSpec(memory_space=pltpu.SMEM),
            pl.BlockSpec(memory_space=pltpu.VMEM),
            pl.BlockSpec(memory_space=pl.ANY),
        ],
        out_specs=tuple(pl.BlockSpec(memory_space=pltpu.VMEM) for _ in range(4)),
        scratch_shapes=[
            V((BLK, B, B), bf16),
            V(cols, bf16), V(cols, bf16), V(cols, bf16),
            V(rows, bf16), V(rows, bf16), V(rows, bf16), V(rows, bf16),
            V(cols, bf16), V(cols, bf16),
            V((BLK + 1, CASES, B), f32),
            V((2 * COLB * CASES, LANES), f32),
            V((2 * COLB, LANES), f32),
            V(half, bf16), V(half, bf16),
            V((4, *ring), bf16), V((4, *ring), bf16), V((4, *ring), bf16),
            pltpu.SemaphoreType.DMA((COPIES,)),
            pltpu.SemaphoreType.DMA((COPIES,)),
            pltpu.SemaphoreType.DMA,
        ],
        compiler_params=pltpu.CompilerParams(
            collective_id=0, has_side_effects=True, vmem_limit_bytes=40 << 20
        ),
    )(table, scale, strengths, blocks)


def solution(mesh):
    in_specs = (
        P("panel", "case"),
        P(("panel", "case"), None, None),
        P(("panel", "case"), None),
        P(),
    )
    out_specs = (P("case", "panel"), P("panel", "case"), P("case", "panel"), P("panel", "case"))
    return jax.shard_map(shards, mesh=mesh, in_specs=in_specs, out_specs=out_specs, check_vma=False)
```

```python
import jax
import jax.numpy as jnp
from jax import lax
from jax.experimental import pallas as pl
from jax.experimental.pallas import tpu as pltpu
from jax.sharding import PartitionSpec as P

B = 256
ROWB = 24
COLB = 48
BLK = 32
CASES = 32
LANES = 128
PART = 3
RING = 8
MESH = pl.DeviceIdType.MESH
FAR_FIRST = (4, 3, 5, 2, 6, 1, 7)
NEAR_FIRST = (1, 7, 2, 6, 3, 5, 4)

f32 = jnp.float32
bf16 = jnp.bfloat16


def chunk(ref, q, count=1):
    return ref.at[pl.ds(q * PART, count * PART)]


def read(ref, q):
    return ref[pl.ds(q * PART, PART)].astype(f32)


def repeat(count, body, unroll=8):
    def some(step, carry):
        for n in range(unroll):
            body(step * unroll + n)
        return carry

    lax.fori_loop(0, count // unroll, some, 0)


class Link:
    def __init__(self, send_sem, recv_sem):
        self.send_sem, self.recv_sem = send_sem, recv_sem
        self.used = 0
        self.open = []

    def take(self, count):
        first = self.used
        self.used += count
        return first

    def copy(self, src, dst, slot_out, slot_in, device):
        return pltpu.make_async_remote_copy(
            src_ref=src,
            dst_ref=dst,
            send_sem=self.send_sem.at[slot_out],
            recv_sem=self.recv_sem.at[slot_in],
            device_id=device,
            device_id_type=MESH,
        )

    def send(self, src, dst, slot_out, slot_in, device):
        copy = self.copy(src, dst, slot_out, slot_in, device)
        copy.start()
        self.open.append(copy)

    def arrived(self, dst, slot_in, device):
        self.copy(dst, dst, slot_in, slot_in, device).wait_recv()

    def drain(self):
        for copy in self.open:
            copy.wait_send()
        self.open = []


class Group:
    def __init__(self, ring, pair, core=None):
        (self.i, self.peer), (self.j, self.partner) = ring, pair
        self.core, self.twin = core if core else (None, None)
        self.base = 0 if core is None else self.core * 16

    def at(self, d):
        return lax.rem(self.i + d, RING)


def gather(link, g, buf, meanwhile=None):
    own_ring = g.base + g.j * RING
    far_ring = g.base + (1 - g.j) * RING
    ring, pair = link.take(RING), link.take(RING)
    twin = link.take(2) if g.twin is not None else None
    mine = chunk(buf, own_ring + g.i)
    link.send(mine, mine, pair, pair, g.partner)
    for d in NEAR_FIRST:
        link.send(mine, mine, ring + d, ring + RING - d, g.peer(d))
    if meanwhile is not None:
        meanwhile()
    for d in NEAR_FIRST:
        piece = chunk(buf, own_ring + g.at(d))
        link.arrived(piece, ring + d, g.peer(d))
        link.send(piece, piece, pair + d, pair + d, g.partner)
    if twin is not None:
        whole = chunk(buf, own_ring, RING)
        link.send(whole, whole, twin, twin, g.twin)
    for d in (0,) + NEAR_FIRST:
        link.arrived(chunk(buf, far_ring + g.at(d)), pair + d, g.partner)
    if twin is not None:
        whole = chunk(buf, far_ring, RING)
        link.send(whole, whole, twin + 1, twin + 1, g.twin)
        other = (1 - g.core) * 16
        link.arrived(chunk(buf, other + g.j * RING, RING), twin, g.twin)
        link.arrived(chunk(buf, other + (1 - g.j) * RING, RING), twin + 1, g.twin)


def scatter(link, g, src, from_twin, joined, from_pair, summed, from_ring, ready_half=None, meanwhile=None):
    if g.twin is not None:
        slots = link.take(2)
        other = (1 - g.core) * 16
        for n, half in enumerate((1 - g.j, g.j)):
            if ready_half is not None:
                ready_half((other + half * RING) * PART)
            link.send(
                chunk(src, other + half * RING, RING),
                chunk(from_twin, half * RING, RING),
                slots + n,
                slots + n,
                g.twin,
            )

        def join(half):
            def one(t):
                at = half * RING * PART + t
                joined[at] = (
                    src[g.base * PART + at].astype(f32) + from_twin[at].astype(f32)
                ).astype(bf16)

            repeat(RING * PART, one)

        if ready_half is not None:
            ready_half((g.base + (1 - g.j) * RING) * PART)
            ready_half((g.base + g.j * RING) * PART)
        link.arrived(chunk(from_twin, (1 - g.j) * RING, RING), slots, g.twin)
        join(1 - g.j)
    ready = src if g.twin is None else joined
    pair, ring = link.take(RING), link.take(RING)
    far, near = (1 - g.j) * RING, g.j * RING
    for d in FAR_FIRST + (0,):
        link.send(chunk(ready, far + g.at(d)), chunk(from_pair, d), pair + d, pair + d, g.partner)
    if g.twin is not None:
        link.arrived(chunk(from_twin, g.j * RING, RING), slots + 1, g.twin)
        join(g.j)
    if meanwhile is not None:
        meanwhile()
    for d in FAR_FIRST:
        link.arrived(chunk(from_pair, d), pair + d, g.partner)
        total = read(ready, near + g.at(d)) + read(from_pair, d)
        summed[pl.ds(d * PART, PART)] = total.astype(bf16)
        link.send(
            chunk(summed, d), chunk(from_ring, RING - d), ring + d, ring + RING - d, g.peer(d)
        )
    link.arrived(chunk(from_pair, 0), pair, g.partner)
    total = read(ready, near + g.i) + read(from_pair, 0)
    for d in NEAR_FIRST:
        link.arrived(chunk(from_ring, d), ring + d, g.peer(d))
        total = total + read(from_ring, d)
    return total


def kernel(
    strengths_hbm, blocks_hbm, pattern_hbm, gain_hbm,
    fwd_one, adj_one, fwd_two, adj_two,
    blocks, rows_in, x_one, x_two, f_one, f_two, y_one, y_two, z_one, z_two,
    terms, wide, flat, twin_buf, join_buf, pair_buf, sum_buf, ring_buf,
    strengths, pattern, pattern_at, gain, keys, found_at, scale_row, table, scale,
    send_sem, recv_sem, load_sem,
):
    p, c = lax.axis_index("panel"), lax.axis_index("case")
    z, x_lo, core = p // 4, lax.rem(p // 2, 2), lax.rem(p, 2)
    x_hi, y = c // RING, lax.rem(c, RING)

    by_panel = Group(
        (z, lambda d: {"panel": lax.rem(z + d, RING) * 4 + x_lo * 2 + core}),
        (x_lo, {"panel": z * 4 + (1 - x_lo) * 2 + core}),
        (core, {"panel": z * 4 + x_lo * 2 + (1 - core)}),
    )
    by_case = Group(
        (y, lambda d: {"case": x_hi * RING + lax.rem(y + d, RING)}),
        (x_hi, {"case": (1 - x_hi) * RING + y}),
    )
    barrier = pltpu.get_barrier_semaphore()
    met = [g.peer(d) for d in (4, 3, 5, 2, 6, 1, 7) for g in (by_panel, by_case)]
    met += [by_panel.twin, by_panel.partner, by_case.partner]
    for device in met:
        pl.semaphore_signal(barrier, inc=1, device_id=device, device_id_type=MESH)

    loads = [
        pltpu.make_async_copy(src, dst, load_sem.at[n])
        for n, (src, dst) in enumerate((
            (strengths_hbm, strengths),
            (pattern_hbm, pattern),
            (pattern_hbm, pattern_at),
            (gain_hbm, gain),
            (blocks_hbm, blocks),
        ))
    ]
    for load in loads:
        load.start()
    place = core * 16 + x_lo * RING + z
    terms[BLK] = jnp.zeros((CASES, B), f32)

    loads[0].wait()
    for n in range(COLB * 2):
        flat[n : n + 1, :] = strengths[0:1, n * LANES : (n + 1) * LANES].astype(f32)
    for n in range(PART):
        rows_in[place * PART + n] = flat[n * CASES : (n + 1) * CASES, :].astype(bf16)
    for load in loads[1:4]:
        load.wait()
    pl.semaphore_wait(barrier, len(met))

    def index_tables():
        line = lax.broadcasted_iota(jnp.int32, (8, LANES), 0)
        lane = lax.broadcasted_iota(jnp.int32, (8, LANES), 1)
        keys[...] = lane
        keys[0:1, 0:BLK] = pattern[0:1, :] - p * ROWB
        keys[1:2, 0:BLK] = pattern[1:2, :] - c * COLB
        wanted = keys[...]
        until = jnp.where(line < 2, lane, BLK)
        by_row = (line == 0) | (line == 2)
        last = jnp.full((8, LANES), BLK, jnp.int32)
        for b in range(BLK):
            live = pattern_at[2, b] >= 0
            row = jnp.where(live, pattern_at[0, b] - p * ROWB, -1000)
            col = jnp.where(live, pattern_at[1, b] - c * COLB, -1000)
            hit = (wanted == jnp.where(by_row, row, col)) & (until > b)
            last = jnp.where(hit, b, last)
        found_at[...] = last
        found_at[4:5, 0:BLK] = jnp.maximum(wanted[0:1, 0:BLK], 0)
        found_at[5:6, 0:BLK] = jnp.maximum(wanted[1:2, 0:BLK], 0)
        chosen = jnp.zeros((1, BLK), f32)
        for n in range(gain_hbm.shape[1]):
            chosen = jnp.where(pattern[2:3, :] == n, gain[0, n], chosen)
        scale_row[0:1, 0:BLK] = chosen
        to_scalars = [
            pltpu.make_async_copy(found_at, table, load_sem.at[0]),
            pltpu.make_async_copy(scale_row, scale, load_sem.at[1]),
        ]
        for copy in to_scalars:
            copy.start()
        for copy in to_scalars:
            copy.wait()

    link = Link(send_sem, recv_sem)
    gather(link, by_panel, rows_in, index_tables)

    def widen(t):
        wide[pl.ds(t * CASES, CASES), :] = rows_in[t].astype(f32)

    def turn(t):
        x_one[t] = wide[pl.ds(t, CASES, stride=COLB * 2), :].astype(bf16)

    repeat(COLB * 2, widen)
    repeat(COLB * 2, turn)
    loads[4].wait()

    def product(src, where_from, chained, dims, unroll):
        def some(step, carry):
            found = []
            for n in range(unroll):
                b = step * unroll + n
                at = table[where_from, b] * 2
                operand = jnp.concatenate([src[at], src[at + 1]], axis=1)
                found.append(
                    lax.dot_general(operand, blocks[b], (dims, ((), ())), preferred_element_type=f32)
                    * scale[0, b]
                )
            for n in range(unroll):
                b = step * unroll + n
                terms[b] = found[n] + terms[table[chained, b]]
            return carry

        lax.fori_loop(0, BLK // unroll, some, 0)

    def forward(src, dst):
        product(src, 5, 0, ((1,), (1,)), 8)

        def out(r):
            total = terms[table[2, r]].astype(bf16)
            dst[2 * r] = total[:, :LANES]
            dst[2 * r + 1] = total[:, LANES:]

        repeat(ROWB, out)

    def adjoint(src, dst):
        product(src, 4, 1, ((1,), (0,)), 16)

        def out(r):
            total = terms[table[3, r]]
            if dst is None:
                wide[pl.ds(2 * r, CASES, stride=COLB * 2), :] = total[:, :LANES]
                wide[pl.ds(2 * r + 1, CASES, stride=COLB * 2), :] = total[:, LANES:]
            else:
                total = total.astype(bf16)
                dst[2 * r] = total[:, :LANES]
                dst[2 * r + 1] = total[:, LANES:]

        repeat(COLB, out)

    def pick(src, dst, places, count):
        lane = lax.broadcasted_iota(jnp.int32, (8, CASES), 1)
        line = lax.broadcasted_iota(jnp.int32, (8, CASES), 0)
        chosen = jnp.zeros((8, CASES), f32)
        for n, at in enumerate(places):
            chosen = jnp.where((line == n) & (lane == at), f32(1.0), chosen)
        chosen = chosen.astype(bf16)
        for t in range(count):
            both = jnp.concatenate([src[2 * t], src[2 * t + 1]], axis=1)
            found = jnp.dot(chosen, both, preferred_element_type=f32)
            dst[:, t * B : (t + 1) * B] = found[: len(places)].astype(bf16)

    def place_of(k):
        return lax.rem(k, 2) * 16 + lax.rem(k // 2, 2) * RING + k // 4

    mine = [place_of(2 * c), place_of(2 * c + 1)]

    def reduce_rows(n, src, dst, meanwhile=None):
        total = scatter(
            link, by_case, src, None, None, pair_buf.at[n], sum_buf.at[n], ring_buf.at[n],
            meanwhile=meanwhile,
        )
        dst[pl.ds(c * PART, PART)] = total.astype(bf16)
        gather(link, by_case, dst)

    def reduce_cols(n, src, ready_half, meanwhile):
        return scatter(
            link, by_panel, src, twin_buf.at[n], join_buf.at[n],
            pair_buf.at[2 * n + 1], sum_buf.at[2 * n + 1], ring_buf.at[2 * n + 1],
            ready_half=ready_half, meanwhile=meanwhile,
        )

    forward(x_one, y_one)
    reduce_rows(0, y_one, f_one)
    adjoint(f_one, z_one)
    total = reduce_cols(0, z_one, None, lambda: pick(f_one, fwd_one, mine, ROWB))
    x_two[pl.ds(place * PART, PART)] = total.astype(bf16)
    gather(link, by_panel, x_two)
    forward(x_two, y_two)
    reduce_rows(2, y_two, f_two, lambda: pick(x_two, adj_one, [place], COLB))
    adjoint(f_two, None)

    def narrow(first):
        def one(t):
            z_two[first + t] = wide[pl.ds((first + t) * CASES, CASES), :].astype(bf16)

        repeat(RING * PART, one)

    total = reduce_cols(1, z_two, narrow, lambda: pick(f_two, fwd_two, mine, ROWB))
    for n in range(PART):
        flat[n * CASES : (n + 1) * CASES, :] = total[n]
    for n in range(COLB * 2):
        adj_two[0:1, n * LANES : (n + 1) * LANES] = flat[n : n + 1, :].astype(bf16)
    link.drain()


COPIES = 160
GRANT = 40 << 20


def shards(strengths, blocks, pattern, level_gain):
    V = pltpu.VMEM
    cols = (2 * COLB, CASES, LANES)
    rows = (2 * ROWB, CASES, LANES)
    ring = (RING * PART, CASES, LANES)
    half = (2, 2 * RING * PART, CASES, LANES)
    results = pl.pallas_call(
        kernel,
        out_shape=(
            jax.ShapeDtypeStruct((2, ROWB * B), bf16),
            jax.ShapeDtypeStruct((1, COLB * B), bf16),
            jax.ShapeDtypeStruct((2, ROWB * B), bf16),
            jax.ShapeDtypeStruct((1, COLB * B), bf16),
        ),
        in_specs=[pl.BlockSpec(memory_space=pltpu.HBM)] * 4,
        out_specs=tuple(pl.BlockSpec(memory_space=pltpu.VMEM) for _ in range(4)),
        scratch_shapes=[
            V((BLK, B, B), bf16),
            V(cols, bf16), V(cols, bf16), V(cols, bf16),
            V(rows, bf16), V(rows, bf16), V(rows, bf16), V(rows, bf16),
            V(cols, bf16), V(cols, bf16),
            V((BLK + 1, CASES, B), f32),
            V((2 * COLB * CASES, LANES), f32),
            V((2 * COLB, LANES), f32),
            V(half, bf16), V(half, bf16),
            V((4, *ring), bf16), V((4, *ring), bf16), V((4, *ring), bf16),
            V((1, COLB * B), bf16),
            V((3, BLK), jnp.int32),
            pltpu.SMEM((3, BLK), jnp.int32),
            pltpu.SMEM((1, level_gain.shape[0]), f32),
            V((8, LANES), jnp.int32), V((8, LANES), jnp.int32), V((8, LANES), f32),
            pltpu.SMEM((8, LANES), jnp.int32), pltpu.SMEM((8, LANES), f32),
            pltpu.SemaphoreType.DMA((COPIES,)),
            pltpu.SemaphoreType.DMA((COPIES,)),
            pltpu.SemaphoreType.DMA((5,)),
        ],
        compiler_params=pltpu.CompilerParams(
            collective_id=0, has_side_effects=True, vmem_limit_bytes=GRANT
        ),
    )(*(pltpu.with_memory_space_constraint(a, pltpu.HBM) for a in (strengths, blocks, pattern.T, level_gain[None, :])))

    def hand_over(*refs):
        ins, outs, sem = refs[:4], refs[4:8], refs[8]
        copies = [pltpu.make_async_copy(a, b, sem.at[n]) for n, (a, b) in enumerate(zip(ins, outs))]
        for copy in copies:
            copy.start()
        for copy in copies:
            copy.wait()

    return pl.pallas_call(
        hand_over,
        out_shape=tuple(jax.ShapeDtypeStruct(r.shape, r.dtype) for r in results),
        in_specs=[pl.BlockSpec(memory_space=pltpu.VMEM)] * 4,
        out_specs=tuple(pl.BlockSpec(memory_space=pl.ANY) for _ in results),
        scratch_shapes=[pltpu.SemaphoreType.DMA((4,))],
    )(*(pltpu.with_memory_space_constraint(r, pltpu.VMEM) for r in results))


def solution(mesh):
    in_specs = (
        P("panel", "case"),
        P(("panel", "case"), None, None),
        P(("panel", "case"), None),
        P(),
    )
    out_specs = (P("case", "panel"), P("panel", "case"), P("case", "panel"), P("panel", "case"))
    return jax.shard_map(shards, mesh=mesh, in_specs=in_specs, out_specs=out_specs, check_vma=False)
```

```python
import jax
import jax.numpy as jnp
from jax import lax
from jax.experimental import pallas as pl
from jax.experimental.pallas import tpu as pltpu
from jax.sharding import PartitionSpec as P

B = 256
ROWB = 24
COLB = 48
BLK = 32
CASES = 32
LANES = 128
PART = 3
RING = 8
MESH = pl.DeviceIdType.MESH
FAR_FIRST = (4, 3, 5, 2, 6, 1, 7)
NEAR_FIRST = (1, 7, 2, 6, 3, 5, 4)

f32 = jnp.float32
bf16 = jnp.bfloat16


def chunk(ref, q, count=1):
    return ref.at[pl.ds(q * PART, count * PART)]


def read(ref, q):
    return ref[pl.ds(q * PART, PART)].astype(f32)


def repeat(count, body, unroll=8):
    def some(step, carry):
        for n in range(unroll):
            body(step * unroll + n)
        return carry

    lax.fori_loop(0, count // unroll, some, 0)


class Link:
    def __init__(self, send_sem, recv_sem):
        self.send_sem, self.recv_sem = send_sem, recv_sem
        self.used = 0
        self.open = []

    def take(self, count):
        first = self.used
        self.used += count
        return first

    def copy(self, src, dst, slot_out, slot_in, device):
        return pltpu.make_async_remote_copy(
            src_ref=src,
            dst_ref=dst,
            send_sem=self.send_sem.at[slot_out],
            recv_sem=self.recv_sem.at[slot_in],
            device_id=device,
            device_id_type=MESH,
        )

    def send(self, src, dst, slot_out, slot_in, device):
        copy = self.copy(src, dst, slot_out, slot_in, device)
        copy.start()
        self.open.append(copy)

    def arrived(self, dst, slot_in, device):
        self.copy(dst, dst, slot_in, slot_in, device).wait_recv()

    def drain(self):
        for copy in self.open:
            copy.wait_send()
        self.open = []


class Group:
    def __init__(self, ring, pair, core=None):
        (self.i, self.peer), (self.j, self.partner) = ring, pair
        self.core, self.twin = core if core else (None, None)
        self.base = 0 if core is None else self.core * 16

    def at(self, d):
        return lax.rem(self.i + d, RING)


def gather(link, g, buf, meanwhile=None, before_last=None):
    own_ring = g.base + g.j * RING
    far_ring = g.base + (1 - g.j) * RING
    ring, pair = link.take(RING), link.take(RING)
    twin = link.take(1 + RING) if g.twin is not None else None
    mine = chunk(buf, own_ring + g.i)
    link.send(mine, mine, pair, pair, g.partner)
    for d in NEAR_FIRST:
        link.send(mine, mine, ring + d, ring + RING - d, g.peer(d))
    if meanwhile is not None:
        meanwhile()
    for d in NEAR_FIRST:
        piece = chunk(buf, own_ring + g.at(d))
        link.arrived(piece, ring + d, g.peer(d))
        link.send(piece, piece, pair + d, pair + d, g.partner)
    if twin is not None:
        whole = chunk(buf, own_ring, RING)
        link.send(whole, whole, twin, twin, g.twin)
    for d in (0,) + NEAR_FIRST:
        piece = chunk(buf, far_ring + g.at(d))
        link.arrived(piece, pair + d, g.partner)
        if twin is not None:
            link.send(piece, piece, twin + 1 + d, twin + 1 + d, g.twin)
    if before_last is not None:
        before_last()
    if twin is not None:
        other = (1 - g.core) * 16
        link.arrived(chunk(buf, other + g.j * RING, RING), twin, g.twin)
        for d in (0,) + NEAR_FIRST:
            piece = chunk(buf, other + (1 - g.j) * RING + g.at(d))
            link.arrived(piece, twin + 1 + d, g.twin)


def scatter(link, g, src, from_twin, joined, from_pair, summed, from_ring, ready_half=None, meanwhile=None):
    if g.twin is not None:
        slots = link.take(2)
        other = (1 - g.core) * 16
        for n, half in enumerate((1 - g.j, g.j)):
            if ready_half is not None:
                ready_half((other + half * RING) * PART)
            link.send(
                chunk(src, other + half * RING, RING),
                chunk(from_twin, half * RING, RING),
                slots + n,
                slots + n,
                g.twin,
            )

        def join(half):
            def one(t):
                at = half * RING * PART + t
                joined[at] = (
                    src[g.base * PART + at].astype(f32) + from_twin[at].astype(f32)
                ).astype(bf16)

            repeat(RING * PART, one)

        if ready_half is not None:
            ready_half((g.base + (1 - g.j) * RING) * PART)
            ready_half((g.base + g.j * RING) * PART)
        link.arrived(chunk(from_twin, (1 - g.j) * RING, RING), slots, g.twin)
        join(1 - g.j)
    ready = src if g.twin is None else joined
    pair, ring = link.take(RING), link.take(RING)
    far, near = (1 - g.j) * RING, g.j * RING
    for d in FAR_FIRST + (0,):
        link.send(chunk(ready, far + g.at(d)), chunk(from_pair, d), pair + d, pair + d, g.partner)
    if g.twin is not None:
        link.arrived(chunk(from_twin, g.j * RING, RING), slots + 1, g.twin)
        join(g.j)
    if meanwhile is not None:
        meanwhile()
    for d in FAR_FIRST:
        link.arrived(chunk(from_pair, d), pair + d, g.partner)
        total = read(ready, near + g.at(d)) + read(from_pair, d)
        summed[pl.ds(d * PART, PART)] = total.astype(bf16)
        link.send(
            chunk(summed, d), chunk(from_ring, RING - d), ring + d, ring + RING - d, g.peer(d)
        )
    link.arrived(chunk(from_pair, 0), pair, g.partner)
    total = read(ready, near + g.i) + read(from_pair, 0)
    for d in NEAR_FIRST:
        link.arrived(chunk(from_ring, d), ring + d, g.peer(d))
        total = total + read(from_ring, d)
    return total


def kernel(
    strengths_hbm, blocks_hbm, pattern_hbm, gain_hbm,
    fwd_one, adj_one, fwd_two, adj_two,
    blocks, turned, rows_in, x_one, x_two, f_one, f_two, y_one, y_two, z_one, z_two,
    terms, wide, flat, twin_buf, join_buf, pair_buf, sum_buf, ring_buf,
    strengths, pattern, pattern_at, gain, keys, found_at, scale_row, table, scale,
    send_sem, recv_sem, load_sem,
):
    p, c = lax.axis_index("panel"), lax.axis_index("case")
    z, x_lo, core = p // 4, lax.rem(p // 2, 2), lax.rem(p, 2)
    x_hi, y = c // RING, lax.rem(c, RING)

    by_panel = Group(
        (z, lambda d: {"panel": lax.rem(z + d, RING) * 4 + x_lo * 2 + core}),
        (x_lo, {"panel": z * 4 + (1 - x_lo) * 2 + core}),
        (core, {"panel": z * 4 + x_lo * 2 + (1 - core)}),
    )
    by_case = Group(
        (y, lambda d: {"case": x_hi * RING + lax.rem(y + d, RING)}),
        (x_hi, {"case": (1 - x_hi) * RING + y}),
    )
    barrier = pltpu.get_barrier_semaphore()
    met = [g.peer(d) for d in (4, 3, 5, 2, 6, 1, 7) for g in (by_panel, by_case)]
    met += [by_panel.twin, by_panel.partner, by_case.partner]
    for device in met:
        pl.semaphore_signal(barrier, inc=1, device_id=device, device_id_type=MESH)

    loads = [
        pltpu.make_async_copy(src, dst, load_sem.at[n])
        for n, (src, dst) in enumerate((
            (strengths_hbm, strengths),
            (pattern_hbm, pattern),
            (pattern_hbm, pattern_at),
            (gain_hbm, gain),
            (blocks_hbm, blocks),
        ))
    ]
    for load in loads:
        load.start()
    place = core * 16 + x_lo * RING + z
    terms[BLK] = jnp.zeros((CASES, B), f32)

    loads[0].wait()
    for n in range(COLB * 2):
        flat[n : n + 1, :] = strengths[0:1, n * LANES : (n + 1) * LANES].astype(f32)
    for n in range(PART):
        rows_in[place * PART + n] = flat[n * CASES : (n + 1) * CASES, :].astype(bf16)
    for load in loads[1:4]:
        load.wait()
    pl.semaphore_wait(barrier, len(met))

    def index_tables():
        line = lax.broadcasted_iota(jnp.int32, (8, LANES), 0)
        lane = lax.broadcasted_iota(jnp.int32, (8, LANES), 1)
        keys[...] = lane
        keys[0:1, 0:BLK] = pattern[0:1, :] - p * ROWB
        keys[1:2, 0:BLK] = pattern[1:2, :] - c * COLB
        wanted = keys[...]
        until = jnp.where(line < 2, lane, BLK)
        by_row = (line == 0) | (line == 2)
        last = jnp.full((8, LANES), BLK, jnp.int32)
        for b in range(BLK):
            live = pattern_at[2, b] >= 0
            row = jnp.where(live, pattern_at[0, b] - p * ROWB, -1000)
            col = jnp.where(live, pattern_at[1, b] - c * COLB, -1000)
            hit = (wanted == jnp.where(by_row, row, col)) & (until > b)
            last = jnp.where(hit, b, last)
        found_at[...] = last
        found_at[4:5, 0:BLK] = jnp.maximum(wanted[0:1, 0:BLK], 0)
        found_at[5:6, 0:BLK] = jnp.maximum(wanted[1:2, 0:BLK], 0)
        chosen = jnp.zeros((1, BLK), f32)
        for n in range(gain_hbm.shape[1]):
            chosen = jnp.where(pattern[2:3, :] == n, gain[0, n], chosen)
        scale_row[0:1, 0:BLK] = chosen
        to_scalars = [
            pltpu.make_async_copy(found_at, table, load_sem.at[0]),
            pltpu.make_async_copy(scale_row, scale, load_sem.at[1]),
        ]
        for copy in to_scalars:
            copy.start()
        loads[4].wait()

        def turn_block(b):
            turned[b] = blocks[b].T

        repeat(BLK, turn_block, 1)
        for copy in to_scalars:
            copy.wait()

    def turn_rows(first):
        first = pl.multiple_of(first, 16)

        def widen(t):
            at = first * PART + t
            wide[pl.ds(at * CASES, CASES), :] = rows_in[at].astype(f32)

        def turn(t):
            found = wide[pl.ds(first * COLB * 2 + t, 16, stride=COLB * 2), :]
            x_one[t, pl.ds(first, 16), :] = found.astype(bf16)

        repeat(16 * PART, widen)
        repeat(COLB * 2, turn)

    link = Link(send_sem, recv_sem)
    gather(link, by_panel, rows_in, index_tables, lambda: turn_rows(core * 16))
    turn_rows((1 - core) * 16)

    def product(src, where_from, chained, tiles, unroll=16):
        def some(step, carry):
            found = []
            for n in range(unroll):
                b = step * unroll + n
                at = table[where_from, b] * 2
                operand = jnp.concatenate([src[at], src[at + 1]], axis=1)
                found.append(
                    jnp.dot(operand, tiles[b], preferred_element_type=f32) * scale[0, b]
                )
            for n in range(unroll):
                b = step * unroll + n
                terms[b] = found[n] + terms[table[chained, b]]
            return carry

        lax.fori_loop(0, BLK // unroll, some, 0)

    def forward(src, dst):
        product(src, 5, 0, turned)

        def out(r):
            total = terms[table[2, r]].astype(bf16)
            dst[2 * r] = total[:, :LANES]
            dst[2 * r + 1] = total[:, LANES:]

        repeat(ROWB, out)

    def adjoint(src, dst):
        product(src, 4, 1, blocks)

        def out(r):
            total = terms[table[3, r]]
            if dst is None:
                wide[pl.ds(2 * r, CASES, stride=COLB * 2), :] = total[:, :LANES]
                wide[pl.ds(2 * r + 1, CASES, stride=COLB * 2), :] = total[:, LANES:]
            else:
                total = total.astype(bf16)
                dst[2 * r] = total[:, :LANES]
                dst[2 * r + 1] = total[:, LANES:]

        repeat(COLB, out)

    def pick(src, dst, places, count):
        lane = lax.broadcasted_iota(jnp.int32, (8, CASES), 1)
        line = lax.broadcasted_iota(jnp.int32, (8, CASES), 0)
        chosen = jnp.zeros((8, CASES), f32)
        for n, at in enumerate(places):
            chosen = jnp.where((line == n) & (lane == at), f32(1.0), chosen)
        chosen = chosen.astype(bf16)
        for t in range(count):
            both = jnp.concatenate([src[2 * t], src[2 * t + 1]], axis=1)
            found = jnp.dot(chosen, both, preferred_element_type=f32)
            dst[:, t * B : (t + 1) * B] = found[: len(places)].astype(bf16)

    def place_of(k):
        return lax.rem(k, 2) * 16 + lax.rem(k // 2, 2) * RING + k // 4

    mine = [place_of(2 * c), place_of(2 * c + 1)]

    def reduce_rows(n, src, dst, meanwhile=None):
        total = scatter(
            link, by_case, src, None, None, pair_buf.at[n], sum_buf.at[n], ring_buf.at[n],
            meanwhile=meanwhile,
        )
        dst[pl.ds(c * PART, PART)] = total.astype(bf16)
        gather(link, by_case, dst)

    def reduce_cols(n, src, ready_half, meanwhile):
        return scatter(
            link, by_panel, src, twin_buf.at[n], join_buf.at[n],
            pair_buf.at[2 * n + 1], sum_buf.at[2 * n + 1], ring_buf.at[2 * n + 1],
            ready_half=ready_half, meanwhile=meanwhile,
        )

    forward(x_one, y_one)
    reduce_rows(0, y_one, f_one)
    adjoint(f_one, z_one)
    total = reduce_cols(0, z_one, None, lambda: pick(f_one, fwd_one, mine, ROWB))
    x_two[pl.ds(place * PART, PART)] = total.astype(bf16)
    gather(link, by_panel, x_two)
    forward(x_two, y_two)
    reduce_rows(2, y_two, f_two, lambda: pick(x_two, adj_one, [place], COLB))
    adjoint(f_two, None)

    def narrow(first):
        def one(t):
            z_two[first + t] = wide[pl.ds((first + t) * CASES, CASES), :].astype(bf16)

        repeat(RING * PART, one)

    total = reduce_cols(1, z_two, narrow, lambda: pick(f_two, fwd_two, mine, ROWB))
    for n in range(PART):
        flat[n * CASES : (n + 1) * CASES, :] = total[n]
    for n in range(COLB * 2):
        adj_two[0:1, n * LANES : (n + 1) * LANES] = flat[n : n + 1, :].astype(bf16)
    link.drain()


COPIES = 160
GRANT = 40 << 20


def shards(strengths, blocks, pattern, level_gain):
    V = pltpu.VMEM
    cols = (2 * COLB, CASES, LANES)
    rows = (2 * ROWB, CASES, LANES)
    ring = (RING * PART, CASES, LANES)
    half = (2, 2 * RING * PART, CASES, LANES)
    results = pl.pallas_call(
        kernel,
        out_shape=(
            jax.ShapeDtypeStruct((2, ROWB * B), bf16),
            jax.ShapeDtypeStruct((1, COLB * B), bf16),
            jax.ShapeDtypeStruct((2, ROWB * B), bf16),
            jax.ShapeDtypeStruct((1, COLB * B), bf16),
        ),
        in_specs=[pl.BlockSpec(memory_space=pltpu.HBM)] * 4,
        out_specs=tuple(pl.BlockSpec(memory_space=pltpu.VMEM) for _ in range(4)),
        scratch_shapes=[
            V((BLK, B, B), bf16), V((BLK, B, B), bf16),
            V(cols, bf16), V(cols, bf16), V(cols, bf16),
            V(rows, bf16), V(rows, bf16), V(rows, bf16), V(rows, bf16),
            V(cols, bf16), V(cols, bf16),
            V((BLK + 1, CASES, B), f32),
            V((2 * COLB * CASES, LANES), f32),
            V((2 * COLB, LANES), f32),
            V(half, bf16), V(half, bf16),
            V((4, *ring), bf16), V((4, *ring), bf16), V((4, *ring), bf16),
            V((1, COLB * B), bf16),
            V((3, BLK), jnp.int32),
            pltpu.SMEM((3, BLK), jnp.int32),
            pltpu.SMEM((1, level_gain.shape[0]), f32),
            V((8, LANES), jnp.int32), V((8, LANES), jnp.int32), V((8, LANES), f32),
            pltpu.SMEM((8, LANES), jnp.int32), pltpu.SMEM((8, LANES), f32),
            pltpu.SemaphoreType.DMA((COPIES,)),
            pltpu.SemaphoreType.DMA((COPIES,)),
            pltpu.SemaphoreType.DMA((5,)),
        ],
        compiler_params=pltpu.CompilerParams(
            collective_id=0, has_side_effects=True, vmem_limit_bytes=GRANT
        ),
    )(*(pltpu.with_memory_space_constraint(a, pltpu.HBM) for a in (strengths, blocks, pattern.T, level_gain[None, :])))

    def hand_over(*refs):
        ins, outs, sem = refs[:4], refs[4:8], refs[8]
        copies = [pltpu.make_async_copy(a, b, sem.at[n]) for n, (a, b) in enumerate(zip(ins, outs))]
        for copy in copies:
            copy.start()
        for copy in copies:
            copy.wait()

    return pl.pallas_call(
        hand_over,
        out_shape=tuple(jax.ShapeDtypeStruct(r.shape, r.dtype) for r in results),
        in_specs=[pl.BlockSpec(memory_space=pltpu.VMEM)] * 4,
        out_specs=tuple(pl.BlockSpec(memory_space=pl.ANY) for _ in results),
        scratch_shapes=[pltpu.SemaphoreType.DMA((4,))],
    )(*(pltpu.with_memory_space_constraint(r, pltpu.VMEM) for r in results))


def solution(mesh):
    in_specs = (
        P("panel", "case"),
        P(("panel", "case"), None, None),
        P(("panel", "case"), None),
        P(),
    )
    out_specs = (P("case", "panel"), P("panel", "case"), P("case", "panel"), P("panel", "case"))
    return jax.shard_map(shards, mesh=mesh, in_specs=in_specs, out_specs=out_specs, check_vma=False)
```

```python
import jax
import jax.numpy as jnp
from jax import lax
from jax.experimental import pallas as pl
from jax.experimental.pallas import tpu as pltpu
from jax.sharding import PartitionSpec as P

B = 256
ROWB = 24
COLB = 48
BLK = 32
CASES = 32
LANES = 128
PART = 3
RING = 8
MESH = pl.DeviceIdType.MESH
FAR_FIRST = (4, 3, 5, 2, 6, 1, 7)
NEAR_FIRST = (1, 7, 2, 6, 3, 5, 4)
FAR = (4, 3, 5)

f32 = jnp.float32
bf16 = jnp.bfloat16


def chunk(ref, q, count=1):
    return ref.at[pl.ds(q * PART, count * PART)]


def read(ref, q):
    return ref[pl.ds(q * PART, PART)].astype(f32)


def repeat(count, body, unroll=8):
    def some(step, carry):
        for n in range(unroll):
            body(step * unroll + n)
        return carry

    lax.fori_loop(0, count // unroll, some, 0)


class Link:
    def __init__(self, send_sem, recv_sem):
        self.send_sem, self.recv_sem = send_sem, recv_sem
        self.used = 0
        self.open = []

    def take(self, count):
        first = self.used
        self.used += count
        return first

    def copy(self, src, dst, slot_out, slot_in, device):
        return pltpu.make_async_remote_copy(
            src_ref=src,
            dst_ref=dst,
            send_sem=self.send_sem.at[slot_out],
            recv_sem=self.recv_sem.at[slot_in],
            device_id=device,
            device_id_type=MESH,
        )

    def send(self, src, dst, slot_out, slot_in, device):
        copy = self.copy(src, dst, slot_out, slot_in, device)
        copy.start()
        self.open.append(copy)

    def arrived(self, dst, slot_in, device):
        self.copy(dst, dst, slot_in, slot_in, device).wait_recv()

    def drain(self):
        for copy in self.open:
            copy.wait_send()
        self.open = []


class Group:
    def __init__(self, ring, pair, core=None):
        (self.i, self.peer), (self.j, self.partner) = ring, pair
        self.core, self.twin = core if core else (None, None)
        self.base = 0 if core is None else self.core * 16

    def at(self, d):
        return lax.rem(self.i + d, RING)


def gather(link, g, buf, meanwhile=None, before_last=None):
    own_ring = g.base + g.j * RING
    far_ring = g.base + (1 - g.j) * RING
    ring, pair = link.take(RING), link.take(RING)
    twin = link.take(1 + RING) if g.twin is not None else None
    mine = chunk(buf, own_ring + g.i)
    link.send(mine, mine, pair, pair, g.partner)
    for d in NEAR_FIRST:
        link.send(mine, mine, ring + d, ring + RING - d, g.peer(d))
    if meanwhile is not None:
        meanwhile()
    for d in NEAR_FIRST[:2]:
        piece = chunk(buf, own_ring + g.at(d))
        link.arrived(piece, ring + d, g.peer(d))
        link.send(piece, piece, pair + d, pair + d, g.partner)
    across = chunk(buf, far_ring + g.i)
    link.arrived(across, pair, g.partner)
    for d in FAR:
        link.send(across, across, pair + d, pair + RING - d, g.peer(d))
    for d in NEAR_FIRST[2:]:
        piece = chunk(buf, own_ring + g.at(d))
        link.arrived(piece, ring + d, g.peer(d))
        if d not in FAR:
            link.send(piece, piece, pair + d, pair + d, g.partner)
    if twin is not None:
        whole = chunk(buf, own_ring, RING)
        link.send(whole, whole, twin, twin, g.twin)
        link.send(across, across, twin + 1, twin + 1, g.twin)
    for d in NEAR_FIRST:
        piece = chunk(buf, far_ring + g.at(d))
        link.arrived(piece, pair + d, g.peer(d) if d in FAR else g.partner)
        if twin is not None:
            link.send(piece, piece, twin + 1 + d, twin + 1 + d, g.twin)
    if before_last is not None:
        before_last()
    if twin is not None:
        other = (1 - g.core) * 16
        link.arrived(chunk(buf, other + g.j * RING, RING), twin, g.twin)
        for d in (0,) + NEAR_FIRST:
            piece = chunk(buf, other + (1 - g.j) * RING + g.at(d))
            link.arrived(piece, twin + 1 + d, g.twin)


def scatter(link, g, src, from_twin, joined, from_pair, summed, from_ring, ready_half=None, meanwhile=None):
    if g.twin is not None:
        slots = link.take(2)
        other = (1 - g.core) * 16
        for n, half in enumerate((1 - g.j, g.j)):
            if ready_half is not None:
                ready_half((other + half * RING) * PART)
            link.send(
                chunk(src, other + half * RING, RING),
                chunk(from_twin, half * RING, RING),
                slots + n,
                slots + n,
                g.twin,
            )

        def join(half):
            def one(t):
                at = half * RING * PART + t
                joined[at] = (
                    src[g.base * PART + at].astype(f32) + from_twin[at].astype(f32)
                ).astype(bf16)

            repeat(RING * PART, one)

        if ready_half is not None:
            ready_half((g.base + (1 - g.j) * RING) * PART)
            ready_half((g.base + g.j * RING) * PART)
        link.arrived(chunk(from_twin, (1 - g.j) * RING, RING), slots, g.twin)
        join(1 - g.j)
    ready = src if g.twin is None else joined
    pair, ring = link.take(RING), link.take(RING)
    far, near = (1 - g.j) * RING, g.j * RING
    for d in FAR_FIRST + (0,):
        link.send(chunk(ready, far + g.at(d)), chunk(from_pair, d), pair + d, pair + d, g.partner)
    if g.twin is not None:
        link.arrived(chunk(from_twin, g.j * RING, RING), slots + 1, g.twin)
        join(g.j)
    if meanwhile is not None:
        meanwhile()
    for d in FAR_FIRST:
        link.arrived(chunk(from_pair, d), pair + d, g.partner)
        total = read(ready, near + g.at(d)) + read(from_pair, d)
        summed[pl.ds(d * PART, PART)] = total.astype(bf16)
        link.send(
            chunk(summed, d), chunk(from_ring, RING - d), ring + d, ring + RING - d, g.peer(d)
        )
    link.arrived(chunk(from_pair, 0), pair, g.partner)
    total = read(ready, near + g.i) + read(from_pair, 0)
    for d in NEAR_FIRST:
        link.arrived(chunk(from_ring, d), ring + d, g.peer(d))
        total = total + read(from_ring, d)
    return total


def kernel(
    strengths_hbm, blocks_hbm, pattern_hbm, gain_hbm,
    fwd_one, adj_one, fwd_two, adj_two,
    blocks, turned, rows_in, x_one, x_two, f_one, f_two, y_one, y_two, z_one, z_two,
    terms, wide, flat, twin_buf, join_buf, pair_buf, sum_buf, ring_buf,
    strengths, pattern, pattern_at, gain, keys, found_at, scale_row, table, scale,
    send_sem, recv_sem, load_sem,
):
    p, c = lax.axis_index("panel"), lax.axis_index("case")
    z, x_lo, core = p // 4, lax.rem(p // 2, 2), lax.rem(p, 2)
    x_hi, y = c // RING, lax.rem(c, RING)

    by_panel = Group(
        (z, lambda d: {"panel": lax.rem(z + d, RING) * 4 + x_lo * 2 + core}),
        (x_lo, {"panel": z * 4 + (1 - x_lo) * 2 + core}),
        (core, {"panel": z * 4 + x_lo * 2 + (1 - core)}),
    )
    by_case = Group(
        (y, lambda d: {"case": x_hi * RING + lax.rem(y + d, RING)}),
        (x_hi, {"case": (1 - x_hi) * RING + y}),
    )
    barrier = pltpu.get_barrier_semaphore()
    met = [g.peer(d) for d in (4, 3, 5, 2, 6, 1, 7) for g in (by_panel, by_case)]
    met += [by_panel.twin, by_panel.partner, by_case.partner]
    for device in met:
        pl.semaphore_signal(barrier, inc=1, device_id=device, device_id_type=MESH)

    loads = [
        pltpu.make_async_copy(src, dst, load_sem.at[n])
        for n, (src, dst) in enumerate((
            (strengths_hbm, strengths),
            (pattern_hbm, pattern),
            (pattern_hbm, pattern_at),
            (gain_hbm, gain),
            (blocks_hbm, blocks),
        ))
    ]
    for load in loads:
        load.start()
    place = core * 16 + x_lo * RING + z
    terms[BLK] = jnp.zeros((CASES, B), f32)

    loads[0].wait()
    for n in range(COLB * 2):
        flat[n : n + 1, :] = strengths[0:1, n * LANES : (n + 1) * LANES].astype(f32)
    for n in range(PART):
        rows_in[place * PART + n] = flat[n * CASES : (n + 1) * CASES, :].astype(bf16)
    for load in loads[1:4]:
        load.wait()
    pl.semaphore_wait(barrier, len(met))

    def index_tables():
        line = lax.broadcasted_iota(jnp.int32, (8, LANES), 0)
        lane = lax.broadcasted_iota(jnp.int32, (8, LANES), 1)
        keys[...] = lane
        keys[0:1, 0:BLK] = pattern[0:1, :] - p * ROWB
        keys[1:2, 0:BLK] = pattern[1:2, :] - c * COLB
        wanted = keys[...]
        until = jnp.where(line < 2, lane, BLK)
        by_row = (line == 0) | (line == 2)
        last = jnp.full((8, LANES), BLK, jnp.int32)
        for b in range(BLK):
            live = pattern_at[2, b] >= 0
            row = jnp.where(live, pattern_at[0, b] - p * ROWB, -1000)
            col = jnp.where(live, pattern_at[1, b] - c * COLB, -1000)
            hit = (wanted == jnp.where(by_row, row, col)) & (until > b)
            last = jnp.where(hit, b, last)
        found_at[...] = last
        found_at[4:5, 0:BLK] = jnp.maximum(wanted[0:1, 0:BLK], 0)
        found_at[5:6, 0:BLK] = jnp.maximum(wanted[1:2, 0:BLK], 0)
        chosen = jnp.zeros((1, BLK), f32)
        for n in range(gain_hbm.shape[1]):
            chosen = jnp.where(pattern[2:3, :] == n, gain[0, n], chosen)
        scale_row[0:1, 0:BLK] = chosen
        to_scalars = [
            pltpu.make_async_copy(found_at, table, load_sem.at[0]),
            pltpu.make_async_copy(scale_row, scale, load_sem.at[1]),
        ]
        for copy in to_scalars:
            copy.start()
        loads[4].wait()

        def turn_block(b):
            turned[b] = blocks[b].T

        repeat(BLK, turn_block, 1)
        for copy in to_scalars:
            copy.wait()

    def turn_rows(first):
        first = pl.multiple_of(first, 16)

        def widen(t):
            at = first * PART + t
            wide[pl.ds(at * CASES, CASES), :] = rows_in[at].astype(f32)

        def turn(t):
            found = wide[pl.ds(first * COLB * 2 + t, 16, stride=COLB * 2), :]
            x_one[t, pl.ds(first, 16), :] = found.astype(bf16)

        repeat(16 * PART, widen)
        repeat(COLB * 2, turn)

    link = Link(send_sem, recv_sem)
    gather(link, by_panel, rows_in, index_tables, lambda: turn_rows(core * 16))
    turn_rows((1 - core) * 16)

    def product(src, where_from, chained, tiles, unroll=16):
        def some(step, carry):
            found = []
            for n in range(unroll):
                b = step * unroll + n
                at = table[where_from, b] * 2
                operand = jnp.concatenate([src[at], src[at + 1]], axis=1)
                found.append(
                    jnp.dot(operand, tiles[b], preferred_element_type=f32) * scale[0, b]
                )
            for n in range(unroll):
                b = step * unroll + n
                terms[b] = found[n] + terms[table[chained, b]]
            return carry

        lax.fori_loop(0, BLK // unroll, some, 0)

    def forward(src, dst):
        product(src, 5, 0, turned)

        def out(r):
            total = terms[table[2, r]].astype(bf16)
            dst[2 * r] = total[:, :LANES]
            dst[2 * r + 1] = total[:, LANES:]

        repeat(ROWB, out)

    def adjoint(src, dst):
        product(src, 4, 1, blocks)

        def out(r):
            total = terms[table[3, r]]
            if dst is None:
                wide[pl.ds(2 * r, CASES, stride=COLB * 2), :] = total[:, :LANES]
                wide[pl.ds(2 * r + 1, CASES, stride=COLB * 2), :] = total[:, LANES:]
            else:
                total = total.astype(bf16)
                dst[2 * r] = total[:, :LANES]
                dst[2 * r + 1] = total[:, LANES:]

        repeat(COLB, out)

    def pick(src, dst, places, count):
        lane = lax.broadcasted_iota(jnp.int32, (8, CASES), 1)
        line = lax.broadcasted_iota(jnp.int32, (8, CASES), 0)
        chosen = jnp.zeros((8, CASES), f32)
        for n, at in enumerate(places):
            chosen = jnp.where((line == n) & (lane == at), f32(1.0), chosen)
        chosen = chosen.astype(bf16)
        for t in range(count):
            both = jnp.concatenate([src[2 * t], src[2 * t + 1]], axis=1)
            found = jnp.dot(chosen, both, preferred_element_type=f32)
            dst[:, t * B : (t + 1) * B] = found[: len(places)].astype(bf16)

    def place_of(k):
        return lax.rem(k, 2) * 16 + lax.rem(k // 2, 2) * RING + k // 4

    mine = [place_of(2 * c), place_of(2 * c + 1)]

    def reduce_rows(n, src, dst, meanwhile=None):
        total = scatter(
            link, by_case, src, None, None, pair_buf.at[n], sum_buf.at[n], ring_buf.at[n],
            meanwhile=meanwhile,
        )
        dst[pl.ds(c * PART, PART)] = total.astype(bf16)
        gather(link, by_case, dst)

    def reduce_cols(n, src, ready_half, meanwhile):
        return scatter(
            link, by_panel, src, twin_buf.at[n], join_buf.at[n],
            pair_buf.at[2 * n + 1], sum_buf.at[2 * n + 1], ring_buf.at[2 * n + 1],
            ready_half=ready_half, meanwhile=meanwhile,
        )

    forward(x_one, y_one)
    reduce_rows(0, y_one, f_one)
    adjoint(f_one, z_one)
    total = reduce_cols(0, z_one, None, lambda: pick(f_one, fwd_one, mine, ROWB))
    x_two[pl.ds(place * PART, PART)] = total.astype(bf16)
    gather(link, by_panel, x_two)
    forward(x_two, y_two)
    reduce_rows(2, y_two, f_two, lambda: pick(x_two, adj_one, [place], COLB))
    adjoint(f_two, None)

    def narrow(first):
        def one(t):
            z_two[first + t] = wide[pl.ds((first + t) * CASES, CASES), :].astype(bf16)

        repeat(RING * PART, one)

    total = reduce_cols(1, z_two, narrow, lambda: pick(f_two, fwd_two, mine, ROWB))
    for n in range(PART):
        flat[n * CASES : (n + 1) * CASES, :] = total[n]
    for n in range(COLB * 2):
        adj_two[0:1, n * LANES : (n + 1) * LANES] = flat[n : n + 1, :].astype(bf16)
    link.drain()


COPIES = 160
GRANT = 40 << 20


def shards(strengths, blocks, pattern, level_gain):
    V = pltpu.VMEM
    cols = (2 * COLB, CASES, LANES)
    rows = (2 * ROWB, CASES, LANES)
    ring = (RING * PART, CASES, LANES)
    half = (2, 2 * RING * PART, CASES, LANES)
    results = pl.pallas_call(
        kernel,
        out_shape=(
            jax.ShapeDtypeStruct((2, ROWB * B), bf16),
            jax.ShapeDtypeStruct((1, COLB * B), bf16),
            jax.ShapeDtypeStruct((2, ROWB * B), bf16),
            jax.ShapeDtypeStruct((1, COLB * B), bf16),
        ),
        in_specs=[pl.BlockSpec(memory_space=pltpu.HBM)] * 4,
        out_specs=tuple(pl.BlockSpec(memory_space=pltpu.VMEM) for _ in range(4)),
        scratch_shapes=[
            V((BLK, B, B), bf16), V((BLK, B, B), bf16),
            V(cols, bf16), V(cols, bf16), V(cols, bf16),
            V(rows, bf16), V(rows, bf16), V(rows, bf16), V(rows, bf16),
            V(cols, bf16), V(cols, bf16),
            V((BLK + 1, CASES, B), f32),
            V((2 * COLB * CASES, LANES), f32),
            V((2 * COLB, LANES), f32),
            V(half, bf16), V(half, bf16),
            V((4, *ring), bf16), V((4, *ring), bf16), V((4, *ring), bf16),
            V((1, COLB * B), bf16),
            V((3, BLK), jnp.int32),
            pltpu.SMEM((3, BLK), jnp.int32),
            pltpu.SMEM((1, level_gain.shape[0]), f32),
            V((8, LANES), jnp.int32), V((8, LANES), jnp.int32), V((8, LANES), f32),
            pltpu.SMEM((8, LANES), jnp.int32), pltpu.SMEM((8, LANES), f32),
            pltpu.SemaphoreType.DMA((COPIES,)),
            pltpu.SemaphoreType.DMA((COPIES,)),
            pltpu.SemaphoreType.DMA((5,)),
        ],
        compiler_params=pltpu.CompilerParams(
            collective_id=0, has_side_effects=True, vmem_limit_bytes=GRANT
        ),
    )(*(pltpu.with_memory_space_constraint(a, pltpu.HBM) for a in (strengths, blocks, pattern.T, level_gain[None, :])))

    def hand_over(*refs):
        ins, outs, sem = refs[:4], refs[4:8], refs[8]
        copies = [pltpu.make_async_copy(a, b, sem.at[n]) for n, (a, b) in enumerate(zip(ins, outs))]
        for copy in copies:
            copy.start()
        for copy in copies:
            copy.wait()

    return pl.pallas_call(
        hand_over,
        out_shape=tuple(jax.ShapeDtypeStruct(r.shape, r.dtype) for r in results),
        in_specs=[pl.BlockSpec(memory_space=pltpu.VMEM)] * 4,
        out_specs=tuple(pl.BlockSpec(memory_space=pl.ANY) for _ in results),
        scratch_shapes=[pltpu.SemaphoreType.DMA((4,))],
    )(*(pltpu.with_memory_space_constraint(r, pltpu.VMEM) for r in results))


def solution(mesh):
    in_specs = (
        P("panel", "case"),
        P(("panel", "case"), None, None),
        P(("panel", "case"), None),
        P(),
    )
    out_specs = (P("case", "panel"), P("panel", "case"), P("case", "panel"), P("panel", "case"))
    return jax.shard_map(shards, mesh=mesh, in_specs=in_specs, out_specs=out_specs, check_vma=False)
```
